32 devices in a mesh: rows: 4 (over y, x), cols: 8 (over z, core).
Axes of the slice: x: 2, y: 2, z: 4, core: 2. Of those that a mesh axis runs over, the one named last changes fastest.
Arguments:
- embeddings: bfloat16 [4096, 768], P(('rows', 'cols')), may hold values from -6 to 6
- document_cluster_index: int32 [4096], P(('rows', 'cols')), may hold values from 0 to 63, as said below
Outputs:
- max_similarity: float32 [4096], P(('rows', 'cols'))
- histogram: float32 [128], replicated
The draws below stay inside these ranges and needn't reach their ends.
Inputs may be any that keep to these rules, and one draw needn't show every extreme that they name: `document_cluster_index`: cluster r * 16 to (r + 1) * 16 - 1 form row group r. Each device's block of 128 documents names at most 64 documents of any one row group, and exactly 64 of one. The documents that the devices with one index along cols name for one row group hold at most 32 documents of any one cluster, and in every draw some such set holds exactly 32 of one cluster.
All inputs are finite; a program needn't handle non-finite values.
Results may differ from the reference program's by a relative error of at most 0.0014.
Values may be sent and summed in bfloat16 or wider, within the bound.
A program may use at most 64 MiB of HBM per device.

```python
import jax
import jax.numpy as jnp
from jax import lax

D = 768
CAP = 64
GROUP_CLUSTERS = 16
BINS = 128
CLUSTER_DOC_PEAK = 32
DOC_DEV = 128
DOCS = 4096
N_ROWS = 4
N_COLS = 8


def draw_document_cluster_index(key, part):
    row_offset = jax.random.randint(jax.random.fold_in(key, 7), (N_ROWS,), 0, GROUP_CLUSTERS)
    fixed_col = jax.random.randint(jax.random.fold_in(key, 8), (), 0, N_COLS)
    fixed_row = jax.random.randint(jax.random.fold_in(key, 9), (), 0, N_ROWS)
    device_base = jax.random.fold_in(key, 11)
    order_base = jax.random.fold_in(key, 12)
    pool_rows = jnp.arange((N_ROWS - 1) * CAP, dtype=jnp.int32) // CAP

    def one_device(device_index):
        device_key = jax.random.fold_in(device_base, device_index)
        first_row = jax.random.randint(jax.random.fold_in(device_key, 1), (), 0, N_ROWS)
        first_row = jnp.where(device_index % N_COLS == fixed_col, fixed_row, first_row).astype(jnp.int32)
        other_rows = (first_row + 1 + pool_rows) % N_ROWS
        other_rows = jax.random.permutation(jax.random.fold_in(device_key, 2), other_rows)[:DOC_DEV - CAP]
        targets = jnp.concatenate([jnp.full((CAP,), first_row, jnp.int32), other_rows.astype(jnp.int32)])
        return jax.random.permutation(jax.random.fold_in(device_key, 3), targets).astype(jnp.int32)
    targets = jax.vmap(one_device)(jnp.arange(N_ROWS * N_COLS, dtype=jnp.int32))
    column_wise = targets.reshape(N_ROWS, N_COLS, DOC_DEV).transpose(1, 0, 2).reshape(N_COLS, N_ROWS * DOC_DEV)
    onehot = (column_wise[:, :, None] == jnp.arange(N_ROWS, dtype=jnp.int32)[None, None, :]).astype(jnp.int32)
    ranks = jnp.sum((jnp.cumsum(onehot, axis=1) - 1) * onehot, axis=2).astype(jnp.int32)
    pooled_clusters = jnp.arange(GROUP_CLUSTERS * CLUSTER_DOC_PEAK, dtype=jnp.int32) // CLUSTER_DOC_PEAK
    stride_length = max(1, 2 ** 20 // GROUP_CLUSTERS)

    def single_order(order_index):
        row_group = order_index % N_ROWS
        sorting_key = jax.random.fold_in(order_base, order_index)
        current_best = (pooled_clusters - row_offset[row_group]) % GROUP_CLUSTERS
        similarity_scores = jax.random.randint(sorting_key, (GROUP_CLUSTERS * CLUSTER_DOC_PEAK,), 0, 2 ** 20) + current_best * stride_length
        similarity_scores = jnp.where(current_best == 0, -1, similarity_scores)
        return pooled_clusters[jnp.argsort(similarity_scores, stable=True)].astype(jnp.int32)
    order_list = jax.vmap(single_order)(jnp.arange(N_COLS * N_ROWS, dtype=jnp.int32)).reshape(N_COLS, N_ROWS, GROUP_CLUSTERS * CLUSTER_DOC_PEAK)
    cluster_member = order_list[jnp.arange(N_COLS, dtype=jnp.int32)[:, None], column_wise, ranks]
    cluster_labels = column_wise * GROUP_CLUSTERS + cluster_member
    return cluster_labels.reshape(N_COLS, N_ROWS, DOC_DEV).transpose(1, 0, 2).reshape(-1).astype(jnp.int32)


def shard_levels(stream_key, dims, split, least, high):
    def one(axis_at, blocks):
        steps = jax.random.uniform(jax.random.fold_in(jax.random.fold_in(stream_key, 6), axis_at), (blocks,), jnp.float32, least / len(split), high / len(split))
        return jnp.repeat(jnp.exp(steps), dims[axis_at] // blocks).reshape((-1,) + (1,) * (len(dims) - axis_at - 1))

    gain = one(*split[0])
    for cut in split[1:]:
        gain = gain * one(*cut)
    return gain


def noise(rng, shape, scale, limit, split=(), kind=jnp.bfloat16):
    loudness = shard_levels(rng, shape, split, -0.22, 0.18) if split else 1.0
    result = jax.random.normal(rng, shape, jnp.float32) * scale * loudness
    return jnp.minimum(jnp.maximum(result, -limit), limit).astype(kind)


def setup_inputs(seed: int = 0) -> dict:
    arg_keys = jax.random.split(jax.random.key(seed), 3)
    embeddings = noise(arg_keys[0], (DOCS, D), 1.0, 6.0, ((0, 32),))
    document_cluster_index = draw_document_cluster_index(jax.random.fold_in(arg_keys[2], 71), 0)
    return dict(embeddings=embeddings, document_cluster_index=document_cluster_index)


def reference(embeddings, document_cluster_index):
    values = embeddings.astype(jnp.float32)
    normed = (values * lax.rsqrt(lax.optimization_barrier(jnp.sum(values * values, axis=1, keepdims=True)) + 1e-06)).astype(jnp.bfloat16)
    doc_total = document_cluster_index.shape[0]
    owner_devices = (document_cluster_index // GROUP_CLUSTERS).astype(jnp.int32)
    doc_order = jnp.argsort(owner_devices, stable=True).astype(jnp.int32)
    counts = lax.optimization_barrier(jnp.sum((owner_devices[:, None] == jnp.arange(N_ROWS, dtype=jnp.int32)[None, :]).astype(jnp.int32), axis=0))
    starts = (jnp.cumsum(counts) - counts).astype(jnp.int32)
    row_span = CAP * N_ROWS * N_COLS
    tile_rows = min(512, row_span)
    sorted_rows = jnp.concatenate([normed[doc_order].astype(jnp.float32), jnp.zeros((row_span, normed.shape[1]), jnp.float32)], axis=0)
    cluster_labels = jnp.concatenate([document_cluster_index[doc_order].astype(jnp.int32), jnp.full((row_span,), -1, jnp.int32)], axis=0)
    span_index = jnp.arange(row_span, dtype=jnp.int32)

    def per_group(row_group):
        group_rows = lax.dynamic_slice_in_dim(sorted_rows, starts[row_group], row_span, 0)
        group_labels = lax.dynamic_slice_in_dim(cluster_labels, starts[row_group], row_span, 0)
        group_labels = jnp.where(span_index < counts[row_group], group_labels, -1)

        def per_tile(tile_index):
            tile_start = (tile_index * tile_rows).astype(jnp.int32)
            tile = lax.dynamic_slice_in_dim(group_rows, tile_start, tile_rows, 0)
            tile_labels = lax.dynamic_slice_in_dim(group_labels, tile_start, tile_rows, 0)
            similarity_scores = jnp.dot(tile, group_rows.T, precision=lax.Precision.HIGHEST)
            tile_index_rows = tile_start + jnp.arange(tile_rows, dtype=jnp.int32)
            same_cluster = (tile_labels[:, None] == group_labels[None, :]) & (tile_labels[:, None] >= 0)
            same_cluster = same_cluster & (tile_index_rows[:, None] != span_index[None, :])
            return lax.optimization_barrier(jnp.max(jnp.where(same_cluster, similarity_scores, -1.0), axis=1))
        return lax.map(per_tile, jnp.arange(row_span // tile_rows, dtype=jnp.int32)).reshape(row_span)
    results = lax.map(per_group, jnp.arange(N_ROWS, dtype=jnp.int32))
    sorted_owner = owner_devices[doc_order]
    offsets = (jnp.arange(doc_total, dtype=jnp.int32) - starts[sorted_owner]).astype(jnp.int32)
    sorted_values = results[sorted_owner, offsets]
    max_similarity = jnp.zeros((doc_total,), jnp.float32).at[doc_order].set(sorted_values)
    bin_width = 2.0 / (BINS - 1)
    centers = -1.0 + jnp.arange(BINS, dtype=jnp.float32) * bin_width
    bin_weights = jax.nn.relu(1.0 - jnp.abs(max_similarity[:, None] - centers[None, :]) / bin_width)
    histogram = lax.optimization_barrier(jnp.sum(bin_weights, axis=0)) / doc_total
    return (max_similarity, histogram)
```

```python
import functools

import jax
import jax.numpy as jnp
from jax import lax
from jax.experimental import pallas as pl
from jax.experimental.pallas import tpu as pltpu
from jax.sharding import PartitionSpec as P

CAP = 64
GROUP_CLUSTERS = 16
BINS = 128
CORES = 2


def from_partner(value, axis, bit):
    mask = 2**bit
    pairs = [(source, source ^ mask) for source in range(lax.axis_size(axis))]
    return lax.ppermute(value, axis, pairs)


def shards(embeddings, document_cluster_index):
    row_count = lax.axis_size("rows")
    col_count = lax.axis_size("cols")
    doc_count = embeddings.shape[0]
    width = embeddings.shape[1]
    slot_count = CAP * row_count
    values = embeddings.astype(jnp.float32)
    normed = (values * lax.rsqrt(jnp.sum(values * values, axis=1, keepdims=True) + 1e-06)).astype(
        jnp.bfloat16
    )
    owner_devices = document_cluster_index // GROUP_CLUSTERS
    within_cluster = (document_cluster_index % GROUP_CLUSTERS).astype(jnp.float32)
    onehot_rows = (
        owner_devices[:, None] == jnp.arange(row_count, dtype=jnp.int32)[None, :]
    ).astype(jnp.int32)
    slot_ranks = jnp.sum((jnp.cumsum(onehot_rows, axis=0) - 1) * onehot_rows, axis=1)
    places = owner_devices * CAP + slot_ranks
    outgoing = jnp.zeros((slot_count, width), jnp.bfloat16).at[places].set(normed)
    out_labels = (
        jnp.full((slot_count,), -1.0, jnp.float32)
        .at[places]
        .set(within_cluster)
        .astype(jnp.bfloat16)
    )
    resident, res_labels = (
        lax.all_to_all(outgoing, "rows", split_axis=0, concat_axis=0, tiled=True),
        lax.all_to_all(out_labels, "rows", split_axis=0, concat_axis=0, tiled=True),
    )
    home_labels = res_labels.astype(jnp.float32)
    partner_count = max(1, col_count // GROUP_CLUSTERS)
    owned_count = max(1, GROUP_CLUSTERS // col_count)
    slot_quota = 2 * slot_count // GROUP_CLUSTERS // partner_count
    send_total = col_count * owned_count * slot_quota
    local_cluster = res_labels.astype(jnp.int32)
    occupied = local_cluster >= 0
    onehot_clusters = (
        local_cluster[:, None] == jnp.arange(GROUP_CLUSTERS, dtype=jnp.int32)[None, :]
    ).astype(jnp.int32)
    cluster_rank = jnp.sum((jnp.cumsum(onehot_clusters, axis=0) - 1) * onehot_clusters, axis=1)
    member_slot = cluster_rank % partner_count
    cluster_depth = cluster_rank // partner_count
    destination = local_cluster // owned_count * partner_count + member_slot
    send_place = (
        destination * (owned_count * slot_quota)
        + local_cluster % owned_count * slot_quota
        + cluster_depth
    )
    send_place = jnp.where(occupied, send_place, send_total)
    send_rows = (
        jnp.zeros((send_total, width), jnp.bfloat16).at[send_place].set(resident, mode="drop")
    )
    send_labels = (
        jnp.full((send_total,), -1.0, jnp.float32)
        .at[send_place]
        .set(home_labels, mode="drop")
        .astype(jnp.bfloat16)
    )
    got_rows, got_labels = (
        lax.all_to_all(send_rows, "cols", split_axis=0, concat_axis=0, tiled=True),
        lax.all_to_all(send_labels, "cols", split_axis=0, concat_axis=0, tiled=True),
    )
    member_index = lax.axis_index("cols") % partner_count
    gathered_rows, gathered_labels = (got_rows, got_labels)
    for bit in range(partner_count.bit_length() - 1):
        other_rows, other_labels = from_partner((gathered_rows, gathered_labels), "cols", bit)
        upper = member_index // 2**bit % 2 == 1
        gathered_rows = jnp.where(
            upper,
            jnp.concatenate([other_rows, gathered_rows], axis=0),
            jnp.concatenate([gathered_rows, other_rows], axis=0),
        )
        gathered_labels = jnp.where(
            upper,
            jnp.concatenate([other_labels, gathered_labels], axis=0),
            jnp.concatenate([gathered_labels, other_labels], axis=0),
        )
    similarity_scores = lax.dot_general(
        got_rows, gathered_rows, (((1,), (1,)), ((), ())), preferred_element_type=jnp.float32
    )
    own_labels = got_labels.astype(jnp.float32)
    all_labels = gathered_labels.astype(jnp.float32)
    column_index = jnp.arange(gathered_rows.shape[0], dtype=jnp.int32)
    own_index = member_index * send_total + jnp.arange(send_total, dtype=jnp.int32)
    same_cluster = (own_labels[:, None] == all_labels[None, :]) & (own_labels[:, None] >= 0.0)
    same_cluster = same_cluster & (own_index[:, None] != column_index[None, :])
    best_owned = jnp.max(jnp.where(same_cluster, similarity_scores, -1.0), axis=1)
    came_back = lax.all_to_all(best_owned, "cols", split_axis=0, concat_axis=0, tiled=True)
    row_best = jnp.where(occupied, came_back[jnp.minimum(send_place, send_total - 1)], -1.0)
    answers = lax.all_to_all(row_best, "rows", split_axis=0, concat_axis=0, tiled=True)
    max_similarity = answers[places]
    bin_width = 2.0 / (BINS - 1)
    centers = -1.0 + jnp.arange(BINS, dtype=jnp.float32) * bin_width
    bin_weights = jax.nn.relu(1.0 - jnp.abs(max_similarity[:, None] - centers[None, :]) / bin_width)
    bin_totals = lax.psum(jnp.sum(bin_weights, axis=0), ("rows", "cols"))
    return (max_similarity, bin_totals / (doc_count * row_count * col_count))


def plane_kernel(planes, doc_total, emb_ref, cluster_ref, best_ref, hist_ref, keys, send, queries, lab_send, labs,
                 best_send, best_box, hist_send, hist_box, z_sems, hop_sems, core_sems, lab_sems, best_sems, hist_sems):
    row = lax.axis_index("rows")
    col = lax.axis_index("cols")
    z, core = col // CORES, col % CORES
    row_at = (row, row + 1 - 2 * (row % 2), row + 2 - 4 * (row // 2), 3 - row)
    core_at = (core, 1 - core)
    rows = len(row_at)

    def device(m, k, d):
        return (row_at[m], lax.rem(z + d, planes) * CORES + core_at[k])

    peers = [(m, k, d) for d in range(planes) for k in range(CORES) for m in range(rows) if m or k or d]

    def copy(source, target, sems, at, where):
        return pltpu.make_async_remote_copy(
            src_ref=source, dst_ref=target, send_sem=sems.at[(0, *at)], recv_sem=sems.at[(1, *at)],
            device_id=where, device_id_type=pl.DeviceIdType.MESH)

    barrier = pltpu.get_barrier_semaphore()
    for peer in peers:
        pl.semaphore_signal(barrier, inc=1, device_id=device(*peer), device_id_type=pl.DeviceIdType.MESH)

    docs, width = emb_ref.shape
    cluster = cluster_ref[...]
    group = cluster // GROUP_CLUSTERS
    local = (cluster - group * GROUP_CLUSTERS).astype(jnp.float32)
    distance = group - z
    distance = jnp.where(distance < 0, distance + planes, distance)
    member = lax.broadcasted_iota(jnp.int32, (8, docs), 0) == distance
    earlier = lax.broadcasted_iota(jnp.int32, (docs, docs), 0) < lax.broadcasted_iota(jnp.int32, (docs, docs), 1)
    counts = jnp.dot(member.astype(jnp.bfloat16), earlier.astype(jnp.bfloat16), preferred_element_type=jnp.float32)
    rank = jnp.sum(jnp.where(member, counts, 0.0), axis=0, keepdims=True).astype(jnp.int32)
    place = distance * CAP + rank
    onehot = (lax.broadcasted_iota(jnp.int32, (planes * CAP, docs), 0) == place).astype(jnp.bfloat16)
    wide = lax.broadcasted_iota(jnp.int32, (128, docs), 0)
    label_rows = jnp.where(member, local + 1.0, 0.0).astype(jnp.bfloat16)
    label_slots = lax.dot_general(
        label_rows, (wide == rank).astype(jnp.bfloat16), (((1,), (1,)), ((), ())), preferred_element_type=jnp.float32
    ) - 1.0
    values = emb_ref[...].astype(jnp.float32)
    normed = (values * lax.rsqrt(jnp.sum(values * values, axis=1, keepdims=True) + 1e-06)).astype(jnp.bfloat16)
    slots = jnp.dot(onehot, normed, preferred_element_type=jnp.float32).astype(jnp.bfloat16)
    keys[0, 0] = slots[:CAP]
    for d in range(planes):
        lab_send[d] = label_slots[d : d + 1]
        if d:
            send[d - 1] = slots[d * CAP : (d + 1) * CAP]
    labs[0, 0] = label_slots[0:1]

    pl.semaphore_wait(barrier, len(peers))

    here, there = (row, col), (row, z * CORES + core_at[1])
    x_peer, y_peer = (row_at[1], col), (row_at[2], col)
    half = CAP // 2
    low, high = pl.ds(0, half), pl.ds(half, half)

    def along_z(d):
        return copy(send.at[d - 1], keys.at[d, 0], z_sems, (d,), device(0, 0, d))

    def hop(n, d):
        source, target, peer = (
            (keys.at[d, 0], keys.at[d, 1], x_peer),
            (keys.at[d, 0], keys.at[d, 2], y_peer),
            (keys.at[d, 1, low], keys.at[d, 3, low], y_peer),
            (keys.at[d, 2, high], keys.at[d, 3, high], x_peer),
        )[n]
        return copy(source, target, hop_sems, (n, d), peer)

    def across(m, d):
        return copy(keys.at[d, m], keys.at[d, rows + m], core_sems, (m, d), there)

    def label_copy(m, k, d):
        return copy(lab_send.at[d], labs.at[d, k * rows + m], lab_sems, (d, k * rows + m), device(m, k, d))

    def best_copy(d):
        return copy(best_send.at[d // 2], best_box.at[d], best_sems, (d,), (row, lax.rem(z + planes - d, planes) * CORES + core))

    def hist_copy(m, k, d):
        return copy(hist_send, hist_box.at[d, k * rows + m], hist_sems, (d, k * rows + m), device(m, k, d))

    def own(d):
        if d:
            along_z(d).wait_recv()
        hop(0, d).start()
        hop(1, d).start()
        across(0, d).start()

    def forward(d):
        hop(0, d).wait_recv()
        hop(2, d).start()
        across(1, d).start()
        hop(1, d).wait_recv()
        hop(3, d).start()
        across(2, d).start()

    def corner(d):
        hop(2, d).wait_recv()
        hop(3, d).wait_recv()
        across(3, d).start()

    for d in range(1, planes):
        along_z(d).start()
    own(0)
    for peer in peers:
        label_copy(*peer).start()
    for d in range(1, planes):
        own(d)
        forward(d - 1)
    for peer in peers:
        label_copy(*peer).wait_recv()
    corner(0)
    for d in range(planes):
        queries[d * CAP : (d + 1) * CAP, :] = keys[d, 0]
    corner(1)
    lanes = lax.broadcasted_iota(jnp.int32, (CORES * rows, 128), 1)
    tables = [labs[d, :, 0, :] for d in range(planes)]
    query_labels = jnp.concatenate(
        [jnp.where(lanes < CAP, tables[d], pltpu.roll(tables[d + 1], CAP, 1))[0:1] for d in range(0, planes, 2)], axis=1
    )
    query_count = planes * CAP
    key_index = lax.broadcasted_iota(jnp.int32, (CAP, query_count), 0)
    query_index = lax.broadcasted_iota(jnp.int32, (CAP, query_count), 1)
    best = jnp.full((8, query_count), -1.0, jnp.float32)
    for d in range(planes):
        if d == planes - 2:
            forward(planes - 1)
        if d >= planes - 2:
            corner(d)
        for m in range(rows):
            across(m, d).wait_recv()
        block = keys[d].reshape(CORES * rows * CAP, width)
        scores = lax.dot_general(block, queries[...], (((1,), (1,)), ((), ())), preferred_element_type=jnp.float32)
        key_labels = tables[d].T
        for j in range(CORES * rows):
            same = (key_labels[:CAP, j : j + 1] == query_labels) & (query_labels >= 0.0)
            if j == 0:
                same = same & (key_index + d * CAP != query_index)
            part = jnp.where(same, scores[j * CAP : (j + 1) * CAP], -1.0)
            best = jnp.maximum(best, jnp.max(part.reshape(CAP // 8, 8, query_count), axis=0))
    best = jnp.max(best, axis=0, keepdims=True)
    for n in range(planes // 2):
        best_send[n] = best[:, n * 128 : (n + 1) * 128]
    best_box[0] = best[:, :128]
    for d in range(1, planes):
        best_copy(d).start()

    bin_width = 2.0 / (BINS - 1)
    centers = -1.0 + lax.broadcasted_iota(jnp.int32, (BINS, query_count), 0).astype(jnp.float32) * bin_width
    weights = jnp.maximum(1.0 - jnp.abs(best - centers) / bin_width, 0.0)
    filled = jnp.broadcast_to((query_labels >= 0.0).astype(jnp.float32), (8, query_count))
    totals = lax.dot_general(
        filled, weights, (((1,), (1,)), ((), ())), precision=lax.Precision.HIGHEST, preferred_element_type=jnp.float32
    )[0:1]
    hist_send[...] = totals
    hist_box[0, 0] = totals
    for peer in peers:
        hist_copy(*peer).start()

    for d in range(1, planes):
        best_copy(d).wait_recv()
    answers = jnp.concatenate([best_box[d] for d in range(planes)] * (8 // planes), axis=0)
    found = [
        jnp.dot(answers, (wide == rank + n * CAP).astype(jnp.float32), precision=lax.Precision.HIGHEST,
                preferred_element_type=jnp.float32)
        for n in range(2)
    ]
    odd = lax.broadcasted_iota(jnp.int32, (8, docs), 0) % 2 == 1
    best_ref[...] = jnp.sum(jnp.where(member, jnp.where(odd, found[1], found[0]), 0.0), axis=0, keepdims=True)

    for d in range(1, planes):
        along_z(d).wait_send()
        best_copy(d).wait_send()
    for d in range(planes):
        for n in range(4):
            hop(n, d).wait_send()
        for m in range(rows):
            across(m, d).wait_send()
    for peer in peers:
        label_copy(*peer).wait_send()
    for peer in peers:
        hist_copy(*peer).wait()
    hist_ref[...] = jnp.sum(jnp.sum(hist_box[...], axis=0), axis=0) / doc_total


def plane_shards(embeddings, document_cluster_index):
    rows, cols = lax.axis_size("rows"), lax.axis_size("cols")
    planes = cols // CORES
    docs, width = embeddings.shape
    blocks = CORES * rows
    vmem = pl.BlockSpec(memory_space=pltpu.VMEM)
    dma = pltpu.SemaphoreType.DMA
    row = lambda *lead: pltpu.VMEM((*lead, 1, 128), jnp.float32)
    best, histogram = pl.pallas_call(
        functools.partial(plane_kernel, planes, docs * rows * cols),
        out_shape=(jax.ShapeDtypeStruct((1, docs), jnp.float32), jax.ShapeDtypeStruct((1, BINS), jnp.float32)),
        in_specs=[vmem, vmem],
        out_specs=(vmem, vmem),
        scratch_shapes=[
            pltpu.VMEM((planes, blocks, CAP, width), jnp.bfloat16),
            pltpu.VMEM((planes - 1, CAP, width), jnp.bfloat16),
            pltpu.VMEM((planes * CAP, width), jnp.bfloat16),
            row(planes),
            row(planes, blocks),
            row(planes // 2),
            row(planes),
            row(),
            row(planes, blocks),
            dma((2, planes)),
            dma((2, 4, planes)),
            dma((2, rows, planes)),
            dma((2, planes, blocks)),
            dma((2, planes)),
            dma((2, planes, blocks)),
        ],
        compiler_params=pltpu.CompilerParams(collective_id=0, has_side_effects=True),
    )(embeddings, document_cluster_index.reshape(1, docs))
    return best.reshape(docs), histogram.reshape(BINS)


def solution(mesh):
    placed = (P(("rows", "cols"), None), P(("rows", "cols")))
    rows, planes = mesh.shape["rows"], mesh.shape["cols"] // CORES
    direct = rows == 4 and planes == rows
    return jax.shard_map(
        plane_shards if direct else shards, mesh=mesh, in_specs=placed,
        out_specs=(P(("rows", "cols")), P()), check_vma=False
    )
```

```python
import functools

import jax
import jax.numpy as jnp
from jax import lax
from jax.experimental import pallas as pl
from jax.experimental.pallas import tpu as pltpu
from jax.sharding import PartitionSpec as P

CAP = 64
GROUP_CLUSTERS = 16
BINS = 128
CORES = 2


def from_partner(value, axis, bit):
    mask = 2**bit
    pairs = [(source, source ^ mask) for source in range(lax.axis_size(axis))]
    return lax.ppermute(value, axis, pairs)


def shards(embeddings, document_cluster_index):
    row_count = lax.axis_size("rows")
    col_count = lax.axis_size("cols")
    doc_count = embeddings.shape[0]
    width = embeddings.shape[1]
    slot_count = CAP * row_count
    values = embeddings.astype(jnp.float32)
    normed = (values * lax.rsqrt(jnp.sum(values * values, axis=1, keepdims=True) + 1e-06)).astype(
        jnp.bfloat16
    )
    owner_devices = document_cluster_index // GROUP_CLUSTERS
    within_cluster = (document_cluster_index % GROUP_CLUSTERS).astype(jnp.float32)
    onehot_rows = (
        owner_devices[:, None] == jnp.arange(row_count, dtype=jnp.int32)[None, :]
    ).astype(jnp.int32)
    slot_ranks = jnp.sum((jnp.cumsum(onehot_rows, axis=0) - 1) * onehot_rows, axis=1)
    places = owner_devices * CAP + slot_ranks
    outgoing = jnp.zeros((slot_count, width), jnp.bfloat16).at[places].set(normed)
    out_labels = (
        jnp.full((slot_count,), -1.0, jnp.float32)
        .at[places]
        .set(within_cluster)
        .astype(jnp.bfloat16)
    )
    resident, res_labels = (
        lax.all_to_all(outgoing, "rows", split_axis=0, concat_axis=0, tiled=True),
        lax.all_to_all(out_labels, "rows", split_axis=0, concat_axis=0, tiled=True),
    )
    home_labels = res_labels.astype(jnp.float32)
    partner_count = max(1, col_count // GROUP_CLUSTERS)
    owned_count = max(1, GROUP_CLUSTERS // col_count)
    slot_quota = 2 * slot_count // GROUP_CLUSTERS // partner_count
    send_total = col_count * owned_count * slot_quota
    local_cluster = res_labels.astype(jnp.int32)
    occupied = local_cluster >= 0
    onehot_clusters = (
        local_cluster[:, None] == jnp.arange(GROUP_CLUSTERS, dtype=jnp.int32)[None, :]
    ).astype(jnp.int32)
    cluster_rank = jnp.sum((jnp.cumsum(onehot_clusters, axis=0) - 1) * onehot_clusters, axis=1)
    member_slot = cluster_rank % partner_count
    cluster_depth = cluster_rank // partner_count
    destination = local_cluster // owned_count * partner_count + member_slot
    send_place = (
        destination * (owned_count * slot_quota)
        + local_cluster % owned_count * slot_quota
        + cluster_depth
    )
    send_place = jnp.where(occupied, send_place, send_total)
    send_rows = (
        jnp.zeros((send_total, width), jnp.bfloat16).at[send_place].set(resident, mode="drop")
    )
    send_labels = (
        jnp.full((send_total,), -1.0, jnp.float32)
        .at[send_place]
        .set(home_labels, mode="drop")
        .astype(jnp.bfloat16)
    )
    got_rows, got_labels = (
        lax.all_to_all(send_rows, "cols", split_axis=0, concat_axis=0, tiled=True),
        lax.all_to_all(send_labels, "cols", split_axis=0, concat_axis=0, tiled=True),
    )
    member_index = lax.axis_index("cols") % partner_count
    gathered_rows, gathered_labels = (got_rows, got_labels)
    for bit in range(partner_count.bit_length() - 1):
        other_rows, other_labels = from_partner((gathered_rows, gathered_labels), "cols", bit)
        upper = member_index // 2**bit % 2 == 1
        gathered_rows = jnp.where(
            upper,
            jnp.concatenate([other_rows, gathered_rows], axis=0),
            jnp.concatenate([gathered_rows, other_rows], axis=0),
        )
        gathered_labels = jnp.where(
            upper,
            jnp.concatenate([other_labels, gathered_labels], axis=0),
            jnp.concatenate([gathered_labels, other_labels], axis=0),
        )
    similarity_scores = lax.dot_general(
        got_rows, gathered_rows, (((1,), (1,)), ((), ())), preferred_element_type=jnp.float32
    )
    own_labels = got_labels.astype(jnp.float32)
    all_labels = gathered_labels.astype(jnp.float32)
    column_index = jnp.arange(gathered_rows.shape[0], dtype=jnp.int32)
    own_index = member_index * send_total + jnp.arange(send_total, dtype=jnp.int32)
    same_cluster = (own_labels[:, None] == all_labels[None, :]) & (own_labels[:, None] >= 0.0)
    same_cluster = same_cluster & (own_index[:, None] != column_index[None, :])
    best_owned = jnp.max(jnp.where(same_cluster, similarity_scores, -1.0), axis=1)
    came_back = lax.all_to_all(best_owned, "cols", split_axis=0, concat_axis=0, tiled=True)
    row_best = jnp.where(occupied, came_back[jnp.minimum(send_place, send_total - 1)], -1.0)
    answers = lax.all_to_all(row_best, "rows", split_axis=0, concat_axis=0, tiled=True)
    max_similarity = answers[places]
    bin_width = 2.0 / (BINS - 1)
    centers = -1.0 + jnp.arange(BINS, dtype=jnp.float32) * bin_width
    bin_weights = jax.nn.relu(1.0 - jnp.abs(max_similarity[:, None] - centers[None, :]) / bin_width)
    bin_totals = lax.psum(jnp.sum(bin_weights, axis=0), ("rows", "cols"))
    return (max_similarity, bin_totals / (doc_count * row_count * col_count))


def plane_kernel(planes, doc_total, emb_hbm, cluster_hbm, best_ref, hist_ref, emb_ref, cluster_ref, keys, send, queries,
                 lab_send, labs, best_send, best_box, hist_send, hist_box, in_sems, z_sems, hop_sems, core_sems, best_sems,
                 hist_sems):
    row = lax.axis_index("rows")
    col = lax.axis_index("cols")
    z, core = col // CORES, col % CORES
    row_at = (row, row + 1 - 2 * (row % 2), row + 2 - 4 * (row // 2), 3 - row)
    core_at = (core, 1 - core)
    rows = len(row_at)

    def device(m, k, d):
        return (row_at[m], lax.rem(z + d, planes) * CORES + core_at[k])

    peers = [(m, k, d) for d in range(planes) for k in range(CORES) for m in range(rows) if m or k or d]

    def copy(source, target, sems, at, where):
        return pltpu.make_async_remote_copy(
            src_ref=source, dst_ref=target, send_sem=sems.at[(0, *at)], recv_sem=sems.at[(1, *at)],
            device_id=where, device_id_type=pl.DeviceIdType.MESH)

    barrier = pltpu.get_barrier_semaphore()
    greeted = [(0, 0, d) for d in range(1, planes)] + [(1, 0, 0), (2, 0, 0), (0, 1, 0)]
    for peer in greeted:
        pl.semaphore_signal(barrier, inc=1, device_id=device(*peer), device_id_type=pl.DeviceIdType.MESH)
    loads = [pltpu.make_async_copy(emb_hbm, emb_ref, in_sems.at[0]), pltpu.make_async_copy(cluster_hbm, cluster_ref, in_sems.at[1])]
    for load in loads:
        load.start()
    for load in loads:
        load.wait()

    docs, width = emb_ref.shape
    cluster = cluster_ref[...]
    group = cluster // GROUP_CLUSTERS
    local = (cluster - group * GROUP_CLUSTERS).astype(jnp.float32)
    distance = group - z
    distance = jnp.where(distance < 0, distance + planes, distance)
    member = lax.broadcasted_iota(jnp.int32, (8, docs), 0) == distance
    earlier = lax.broadcasted_iota(jnp.int32, (docs, docs), 0) < lax.broadcasted_iota(jnp.int32, (docs, docs), 1)
    counts = jnp.dot(member.astype(jnp.bfloat16), earlier.astype(jnp.bfloat16), preferred_element_type=jnp.float32)
    rank = jnp.sum(jnp.where(member, counts, 0.0), axis=0, keepdims=True).astype(jnp.int32)
    place = distance * CAP + rank
    onehot = (lax.broadcasted_iota(jnp.int32, (planes * CAP, docs), 0) == place).astype(jnp.bfloat16)
    wide = lax.broadcasted_iota(jnp.int32, (128, docs), 0)
    label_rows = jnp.where(member, local + 1.0, 0.0).astype(jnp.bfloat16)
    label_slots = lax.dot_general(
        label_rows, (wide == rank).astype(jnp.bfloat16), (((1,), (1,)), ((), ())), preferred_element_type=jnp.float32
    ) - 1.0
    values = emb_ref[...].astype(jnp.float32)
    normed = (values * lax.rsqrt(jnp.sum(values * values, axis=1, keepdims=True) + 1e-06)).astype(jnp.bfloat16)
    slots = jnp.dot(onehot, normed, preferred_element_type=jnp.float32).astype(jnp.bfloat16)
    keys[0, 0] = slots[:CAP]
    for d in range(1, planes):
        lab_send[d - 1] = label_slots[d : d + 1]
        send[d - 1] = slots[d * CAP : (d + 1) * CAP]
    labs[0, 0] = label_slots[0:1]

    pl.semaphore_wait(barrier, len(greeted))

    here, there = (row, col), (row, z * CORES + core_at[1])
    x_peer, y_peer = (row_at[1], col), (row_at[2], col)
    half = CAP // 2
    low, high = pl.ds(0, half), pl.ds(half, half)

    def slot(d, plane):
        return d if d == 0 else planes - d + (plane % 2) * (2 * d - planes)

    def along_z(d):
        s = slot(d, lax.rem(z + d, planes))
        return [
            copy(lab_send.at[d - 1], labs.at[s, 0], z_sems, (1, s), device(0, 0, d)),
            copy(send.at[d - 1], keys.at[s, 0], z_sems, (0, s), device(0, 0, d)),
        ]

    def from_z(s):
        return [
            copy(lab_send.at[0], labs.at[s, 0], z_sems, (1, s), device(0, 0, 1)),
            copy(send.at[0], keys.at[s, 0], z_sems, (0, s), device(0, 0, 1)),
        ]

    def hop(n, s):
        if n < 2:
            peer = (x_peer, y_peer)[n]
            return [
                copy(labs.at[s, 0], labs.at[s, n + 1], hop_sems, (n, 1, s), peer),
                copy(keys.at[s, 0], keys.at[s, n + 1], hop_sems, (n, 0, s), peer),
            ]
        if n == 2:
            return [
                copy(labs.at[s, 1], labs.at[s, 3], hop_sems, (n, 1, s), y_peer),
                copy(keys.at[s, 1, low], keys.at[s, 3, low], hop_sems, (n, 0, s), y_peer),
            ]
        return [copy(keys.at[s, 2, high], keys.at[s, 3, high], hop_sems, (n, 0, s), x_peer)]

    def across(m, s):
        return [
            copy(labs.at[s, m], labs.at[s, rows + m], core_sems, (m, 1, s), there),
            copy(keys.at[s, m], keys.at[s, rows + m], core_sems, (m, 0, s), there),
        ]

    def start(copies):
        for item in copies:
            item.start()

    def wait_recv(copies):
        for item in copies:
            item.wait_recv()

    def wait_send(copies):
        for item in copies:
            item.wait_send()

    def best_copy(s):
        d = slot(s, z)
        return copy(best_send.at[s // 2], best_box.at[d], best_sems, (d,), (row, lax.rem(z + planes - d, planes) * CORES + core))

    def hist_copy(m, k, d):
        return copy(hist_send, hist_box.at[d, k * rows + m], hist_sems, (d, k * rows + m), device(m, k, d))

    def own(s):
        if s:
            wait_recv(from_z(s))
        start(hop(0, s))
        start(hop(1, s))
        start(across(0, s))

    def forward(s):
        wait_recv(hop(0, s))
        start(hop(2, s))
        start(across(1, s))
        wait_recv(hop(1, s))
        start(hop(3, s))
        start(across(2, s))

    def corner(s):
        wait_recv(hop(2, s))
        wait_recv(hop(3, s))
        start(across(3, s))

    @pl.when(z < planes // 2)
    def _():
        for d in range(planes - 1, 0, -1):
            start(along_z(d))

    @pl.when(z >= planes // 2)
    def _():
        for d in range(1, planes):
            start(along_z(d))

    own(0)
    for s in range(1, planes):
        own(s)
        forward(s - 1)
    corner(0)
    for s in range(planes):
        queries[s * CAP : (s + 1) * CAP, :] = keys[s, 0]
    corner(1)
    lanes = lax.broadcasted_iota(jnp.int32, (1, 128), 1)
    query_tables = [labs[s, 0] for s in range(planes)]
    query_labels = jnp.concatenate(
        [jnp.where(lanes < CAP, query_tables[s], pltpu.roll(query_tables[s + 1], CAP, 1)) for s in range(0, planes, 2)], axis=1
    )
    query_count = planes * CAP
    key_index = lax.broadcasted_iota(jnp.int32, (CAP, query_count), 0)
    query_index = lax.broadcasted_iota(jnp.int32, (CAP, query_count), 1)
    best = jnp.full((8, query_count), -1.0, jnp.float32)
    for d in range(planes):
        if d == planes - 2:
            forward(planes - 1)
        if d >= planes - 2:
            corner(d)
        for m in range(rows):
            wait_recv(across(m, d))
        block = keys[d].reshape(CORES * rows * CAP, width)
        scores = lax.dot_general(block, queries[...], (((1,), (1,)), ((), ())), preferred_element_type=jnp.float32)
        key_labels = labs[d, :, 0, :].T
        for j in range(CORES * rows):
            same = (key_labels[:CAP, j : j + 1] == query_labels) & (query_labels >= 0.0)
            if j == 0:
                same = same & (key_index + d * CAP != query_index)
            part = jnp.where(same, scores[j * CAP : (j + 1) * CAP], -1.0)
            best = jnp.maximum(best, jnp.max(part.reshape(CAP // 8, 8, query_count), axis=0))
    best = jnp.max(best, axis=0, keepdims=True)
    for n in range(planes // 2):
        best_send[n] = best[:, n * 128 : (n + 1) * 128]
    best_box[0] = best[:, :128]
    for d in range(1, planes):
        best_copy(d).start()

    bin_width = 2.0 / (BINS - 1)
    centers = -1.0 + lax.broadcasted_iota(jnp.int32, (BINS, query_count), 0).astype(jnp.float32) * bin_width
    weights = jnp.maximum(1.0 - jnp.abs(best - centers) / bin_width, 0.0)
    filled = jnp.broadcast_to((query_labels >= 0.0).astype(jnp.float32), (8, query_count))
    totals = lax.dot_general(
        filled, weights, (((1,), (1,)), ((), ())), precision=lax.Precision.HIGHEST, preferred_element_type=jnp.float32
    )[0:1]
    hist_send[...] = totals
    hist_box[0, 0] = totals
    for peer in sorted(peers, key=lambda p: -((p[0] > 0) + (p[0] == 3) + (p[2] > 0))):
        hist_copy(*peer).start()

    for d in range(1, planes):
        best_copy(d).wait_recv()
    answers = jnp.concatenate([best_box[d] for d in range(planes)] * (8 // planes), axis=0)
    found = [
        jnp.dot(answers, (wide == rank + n * CAP).astype(jnp.float32), precision=lax.Precision.HIGHEST,
                preferred_element_type=jnp.float32)
        for n in range(2)
    ]
    odd = lax.broadcasted_iota(jnp.int32, (8, docs), 0) % 2 == 1
    best_ref[...] = jnp.sum(jnp.where(member, jnp.where(odd, found[1], found[0]), 0.0), axis=0, keepdims=True)

    for d in range(1, planes):
        wait_send(along_z(d))
        best_copy(d).wait_send()
    for s in range(planes):
        for n in range(4):
            wait_send(hop(n, s))
        for m in range(rows):
            wait_send(across(m, s))
    for peer in peers:
        hist_copy(*peer).wait()
    hist_ref[...] = jnp.sum(jnp.sum(hist_box[...], axis=0), axis=0) / doc_total


def plane_shards(embeddings, document_cluster_index):
    rows, cols = lax.axis_size("rows"), lax.axis_size("cols")
    planes = cols // CORES
    docs, width = embeddings.shape
    blocks = CORES * rows
    hbm, vmem = pl.BlockSpec(memory_space=pl.ANY), pl.BlockSpec(memory_space=pltpu.VMEM)
    dma = pltpu.SemaphoreType.DMA
    row = lambda *lead: pltpu.VMEM((*lead, 1, 128), jnp.float32)
    best, histogram = pl.pallas_call(
        functools.partial(plane_kernel, planes, docs * rows * cols),
        out_shape=(pltpu.VMEM((1, docs), jnp.float32), pltpu.VMEM((1, BINS), jnp.float32)),
        in_specs=[hbm, hbm],
        out_specs=(vmem, vmem),
        scratch_shapes=[
            pltpu.VMEM((docs, width), jnp.bfloat16),
            pltpu.VMEM((1, docs), jnp.int32),
            pltpu.VMEM((planes, blocks, CAP, width), jnp.bfloat16),
            pltpu.VMEM((planes - 1, CAP, width), jnp.bfloat16),
            pltpu.VMEM((planes * CAP, width), jnp.bfloat16),
            row(planes - 1),
            row(planes, blocks),
            row(planes // 2),
            row(planes),
            row(),
            row(planes, blocks),
            dma((2,)),
            dma((2, 2, planes)),
            dma((2, 4, 2, planes)),
            dma((2, rows, 2, planes)),
            dma((2, planes)),
            dma((2, planes, blocks)),
        ],
        compiler_params=pltpu.CompilerParams(collective_id=0, has_side_effects=True),
    )(embeddings, document_cluster_index.reshape(1, docs))
    return best.reshape(docs), histogram.reshape(BINS)


def solution(mesh):
    placed = (P(("rows", "cols"), None), P(("rows", "cols")))
    rows, planes = mesh.shape["rows"], mesh.shape["cols"] // CORES
    direct = rows == 4 and planes == rows
    return jax.shard_map(
        plane_shards if direct else shards, mesh=mesh, in_specs=placed,
        out_specs=(P(("rows", "cols")), P()), check_vma=False
    )
```

```python
import functools

import jax
import jax.numpy as jnp
from jax import lax
from jax.experimental import pallas as pl
from jax.experimental.pallas import tpu as pltpu
from jax.sharding import PartitionSpec as P

CAP = 64
GROUP_CLUSTERS = 16
BINS = 128
CORES = 2


def from_partner(value, axis, bit):
    mask = 2**bit
    pairs = [(source, source ^ mask) for source in range(lax.axis_size(axis))]
    return lax.ppermute(value, axis, pairs)


def shards(embeddings, document_cluster_index):
    row_count = lax.axis_size("rows")
    col_count = lax.axis_size("cols")
    doc_count = embeddings.shape[0]
    width = embeddings.shape[1]
    slot_count = CAP * row_count
    values = embeddings.astype(jnp.float32)
    normed = (values * lax.rsqrt(jnp.sum(values * values, axis=1, keepdims=True) + 1e-06)).astype(
        jnp.bfloat16
    )
    owner_devices = document_cluster_index // GROUP_CLUSTERS
    within_cluster = (document_cluster_index % GROUP_CLUSTERS).astype(jnp.float32)
    onehot_rows = (
        owner_devices[:, None] == jnp.arange(row_count, dtype=jnp.int32)[None, :]
    ).astype(jnp.int32)
    slot_ranks = jnp.sum((jnp.cumsum(onehot_rows, axis=0) - 1) * onehot_rows, axis=1)
    places = owner_devices * CAP + slot_ranks
    outgoing = jnp.zeros((slot_count, width), jnp.bfloat16).at[places].set(normed)
    out_labels = (
        jnp.full((slot_count,), -1.0, jnp.float32)
        .at[places]
        .set(within_cluster)
        .astype(jnp.bfloat16)
    )
    resident, res_labels = (
        lax.all_to_all(outgoing, "rows", split_axis=0, concat_axis=0, tiled=True),
        lax.all_to_all(out_labels, "rows", split_axis=0, concat_axis=0, tiled=True),
    )
    home_labels = res_labels.astype(jnp.float32)
    partner_count = max(1, col_count // GROUP_CLUSTERS)
    owned_count = max(1, GROUP_CLUSTERS // col_count)
    slot_quota = 2 * slot_count // GROUP_CLUSTERS // partner_count
    send_total = col_count * owned_count * slot_quota
    local_cluster = res_labels.astype(jnp.int32)
    occupied = local_cluster >= 0
    onehot_clusters = (
        local_cluster[:, None] == jnp.arange(GROUP_CLUSTERS, dtype=jnp.int32)[None, :]
    ).astype(jnp.int32)
    cluster_rank = jnp.sum((jnp.cumsum(onehot_clusters, axis=0) - 1) * onehot_clusters, axis=1)
    member_slot = cluster_rank % partner_count
    cluster_depth = cluster_rank // partner_count
    destination = local_cluster // owned_count * partner_count + member_slot
    send_place = (
        destination * (owned_count * slot_quota)
        + local_cluster % owned_count * slot_quota
        + cluster_depth
    )
    send_place = jnp.where(occupied, send_place, send_total)
    send_rows = (
        jnp.zeros((send_total, width), jnp.bfloat16).at[send_place].set(resident, mode="drop")
    )
    send_labels = (
        jnp.full((send_total,), -1.0, jnp.float32)
        .at[send_place]
        .set(home_labels, mode="drop")
        .astype(jnp.bfloat16)
    )
    got_rows, got_labels = (
        lax.all_to_all(send_rows, "cols", split_axis=0, concat_axis=0, tiled=True),
        lax.all_to_all(send_labels, "cols", split_axis=0, concat_axis=0, tiled=True),
    )
    member_index = lax.axis_index("cols") % partner_count
    gathered_rows, gathered_labels = (got_rows, got_labels)
    for bit in range(partner_count.bit_length() - 1):
        other_rows, other_labels = from_partner((gathered_rows, gathered_labels), "cols", bit)
        upper = member_index // 2**bit % 2 == 1
        gathered_rows = jnp.where(
            upper,
            jnp.concatenate([other_rows, gathered_rows], axis=0),
            jnp.concatenate([gathered_rows, other_rows], axis=0),
        )
        gathered_labels = jnp.where(
            upper,
            jnp.concatenate([other_labels, gathered_labels], axis=0),
            jnp.concatenate([gathered_labels, other_labels], axis=0),
        )
    similarity_scores = lax.dot_general(
        got_rows, gathered_rows, (((1,), (1,)), ((), ())), preferred_element_type=jnp.float32
    )
    own_labels = got_labels.astype(jnp.float32)
    all_labels = gathered_labels.astype(jnp.float32)
    column_index = jnp.arange(gathered_rows.shape[0], dtype=jnp.int32)
    own_index = member_index * send_total + jnp.arange(send_total, dtype=jnp.int32)
    same_cluster = (own_labels[:, None] == all_labels[None, :]) & (own_labels[:, None] >= 0.0)
    same_cluster = same_cluster & (own_index[:, None] != column_index[None, :])
    best_owned = jnp.max(jnp.where(same_cluster, similarity_scores, -1.0), axis=1)
    came_back = lax.all_to_all(best_owned, "cols", split_axis=0, concat_axis=0, tiled=True)
    row_best = jnp.where(occupied, came_back[jnp.minimum(send_place, send_total - 1)], -1.0)
    answers = lax.all_to_all(row_best, "rows", split_axis=0, concat_axis=0, tiled=True)
    max_similarity = answers[places]
    bin_width = 2.0 / (BINS - 1)
    centers = -1.0 + jnp.arange(BINS, dtype=jnp.float32) * bin_width
    bin_weights = jax.nn.relu(1.0 - jnp.abs(max_similarity[:, None] - centers[None, :]) / bin_width)
    bin_totals = lax.psum(jnp.sum(bin_weights, axis=0), ("rows", "cols"))
    return (max_similarity, bin_totals / (doc_count * row_count * col_count))


def plane_kernel(planes, doc_total, emb_hbm, cluster_hbm, best_ref, hist_ref, emb_ref, cluster_ref, keys, send, queries,
                 lab_send, labs, cross_send, cross_box, best_send, best_box, hist_send, hist_box, in_sems, z_sems, hop_sems, core_sems, cross_sems, best_sems,
                 hist_sems):
    row = lax.axis_index("rows")
    col = lax.axis_index("cols")
    z, core = col // CORES, col % CORES
    row_at = (row, row + 1 - 2 * (row % 2), row + 2 - 4 * (row // 2), 3 - row)
    core_at = (core, 1 - core)
    rows = len(row_at)
    near = rows - 1

    def device(m, k, d):
        return (row_at[m], lax.rem(z + d, planes) * CORES + core_at[k])

    peers = [(m, k, d) for d in range(planes) for k in range(CORES) for m in range(rows) if m or k or d]

    def copy(source, target, sems, at, where):
        return pltpu.make_async_remote_copy(
            src_ref=source, dst_ref=target, send_sem=sems.at[(0, *at)], recv_sem=sems.at[(1, *at)],
            device_id=where, device_id_type=pl.DeviceIdType.MESH)

    barrier = pltpu.get_barrier_semaphore()
    greeted = [(0, 0, d) for d in range(1, planes)] + [(1, 0, 0), (2, 0, 0), (0, 1, 0)]
    for peer in greeted:
        pl.semaphore_signal(barrier, inc=1, device_id=device(*peer), device_id_type=pl.DeviceIdType.MESH)
    loads = [pltpu.make_async_copy(emb_hbm, emb_ref, in_sems.at[0]), pltpu.make_async_copy(cluster_hbm, cluster_ref, in_sems.at[1])]
    for load in loads:
        load.start()
    for load in loads:
        load.wait()

    docs, width = emb_ref.shape
    cluster = cluster_ref[...]
    group = cluster // GROUP_CLUSTERS
    local = (cluster - group * GROUP_CLUSTERS).astype(jnp.float32)
    distance = group - z
    distance = jnp.where(distance < 0, distance + planes, distance)
    member = lax.broadcasted_iota(jnp.int32, (8, docs), 0) == distance
    earlier = lax.broadcasted_iota(jnp.int32, (docs, docs), 0) < lax.broadcasted_iota(jnp.int32, (docs, docs), 1)
    counts = jnp.dot(member.astype(jnp.bfloat16), earlier.astype(jnp.bfloat16), preferred_element_type=jnp.float32)
    rank = jnp.sum(jnp.where(member, counts, 0.0), axis=0, keepdims=True).astype(jnp.int32)
    place = distance * CAP + rank
    onehot = (lax.broadcasted_iota(jnp.int32, (planes * CAP, docs), 0) == place).astype(jnp.bfloat16)
    wide = lax.broadcasted_iota(jnp.int32, (128, docs), 0)
    label_rows = jnp.where(member, local + 1.0, 0.0).astype(jnp.bfloat16)
    label_slots = lax.dot_general(
        label_rows, (wide == rank).astype(jnp.bfloat16), (((1,), (1,)), ((), ())), preferred_element_type=jnp.float32
    ) - 1.0
    values = emb_ref[...].astype(jnp.float32)
    normed = (values * lax.rsqrt(jnp.sum(values * values, axis=1, keepdims=True) + 1e-06)).astype(jnp.bfloat16)
    slots = jnp.dot(onehot, normed, preferred_element_type=jnp.float32).astype(jnp.bfloat16)
    keys[0, 0] = slots[:CAP]
    for d in range(1, planes):
        lab_send[d - 1] = label_slots[d : d + 1]
        send[d - 1] = slots[d * CAP : (d + 1) * CAP]
    labs[0, 0] = label_slots[0:1]
    for s in range(planes):
        for j in range(CORES * near, 8):
            labs[s, j] = jnp.full((1, 128), -1.0, jnp.float32)

    pl.semaphore_wait(barrier, len(greeted))

    here, there = (row, col), (row, z * CORES + core_at[1])
    x_peer, y_peer = (row_at[1], col), (row_at[2], col)
    half = CAP // 2
    low, high = pl.ds(0, half), pl.ds(half, half)

    def slot(d, plane):
        return d if d == 0 else planes - d + (plane % 2) * (2 * d - planes)

    def z_copies(source, target, where):
        return [
            copy(lab_send.at[source], labs.at[target, 0], z_sems, (2, target), where),
            copy(send.at[source, low], keys.at[target, 0, low], z_sems, (0, target), where),
            copy(send.at[source, high], keys.at[target, 0, high], z_sems, (1, target), where),
        ]

    def along_z(d):
        return z_copies(d - 1, slot(d, lax.rem(z + d, planes)), device(0, 0, d))

    def from_z(s):
        return z_copies(0, s, device(0, 0, 1))

    def hop(n, s):
        source, target, part, peer = (
            (0, 1, low, x_peer),
            (0, 1, high, x_peer),
            (0, 2, high, y_peer),
            (0, 2, low, y_peer),
        )[n]
        rest = [copy(keys.at[s, source, part], keys.at[s, target, part], hop_sems, (n, 0, s), peer)]
        if n % 2 == 0:
            rest = [copy(labs.at[s, source], labs.at[s, target], hop_sems, (n, 1, s), peer)] + rest
        return rest

    def across(m, s):
        return [
            copy(labs.at[s, m], labs.at[s, near + m], core_sems, (m, 1, s), there),
            copy(keys.at[s, m], keys.at[s, near + m], core_sems, (m, 0, s), there),
        ]

    def start(copies):
        for item in copies:
            item.start()

    def wait_recv(copies):
        for item in copies:
            item.wait_recv()

    def wait_send(copies):
        for item in copies:
            item.wait_send()

    def best_copy(s):
        d = slot(s, z)
        return copy(best_send.at[s // 2], best_box.at[d], best_sems, (d,), (row, lax.rem(z + planes - d, planes) * CORES + core))

    def hist_copy(m, k, d):
        return copy(hist_send, hist_box.at[d, k * rows + m], hist_sems, (d, k * rows + m), device(m, k, d))

    def own(s):
        first, second = [], []
        if s:
            came = from_z(s)
            first, second = came[:2], came[2:]
        wait_recv(first)
        start(hop(0, s))
        start(hop(3, s))
        wait_recv(second)
        start(hop(2, s))
        start(hop(1, s))
        start(across(0, s))

    def forward(s):
        wait_recv(hop(0, s) + hop(1, s))
        start(across(1, s))
        wait_recv(hop(2, s) + hop(3, s))
        start(across(2, s))

    def cross_copy(n):
        return copy(cross_send.at[n], cross_box.at[n], cross_sems, (n,), (x_peer, y_peer)[n])

    @pl.when(z < planes // 2)
    def _():
        for d in range(planes - 1, 0, -1):
            start(along_z(d))

    @pl.when(z >= planes // 2)
    def _():
        for d in range(1, planes):
            start(along_z(d))

    own(0)
    for s in range(1, planes):
        own(s)
        forward(s - 1)
    last = planes - 1
    query_count = planes * CAP
    lanes = lax.broadcasted_iota(jnp.int32, (1, 128), 1)
    key_index = lax.broadcasted_iota(jnp.int32, (CAP, query_count), 0)
    query_index = lax.broadcasted_iota(jnp.int32, (CAP, query_count), 1)

    def collect(n, j, s):
        queries[n, s * CAP : (s + 1) * CAP, :] = keys[s, j]

    def labels_of(j):
        pieces = [labs[s, j] for s in range(planes)]
        return jnp.concatenate(
            [jnp.where(lanes < CAP, pieces[s], pltpu.roll(pieces[s + 1], CAP, 1)) for s in range(0, planes, 2)], axis=1
        )

    def compare(best, block, key_labels, query, query_labels, skip):
        scores = lax.dot_general(block, query, (((1,), (1,)), ((), ())), preferred_element_type=jnp.float32)
        for i, column in enumerate(key_labels):
            same = (column == query_labels) & (query_labels >= 0.0)
            if i == 0 and skip is not None:
                same = same & (key_index + skip * CAP != query_index)
            part = jnp.where(same, scores[i * CAP : (i + 1) * CAP], -1.0)
            best = jnp.maximum(best, jnp.max(part.reshape(CAP // 8, 8, query_count), axis=0))
        return best

    def own_group(best, s, query_labels):
        block = keys[s].reshape(CORES * near * CAP, width)
        table = labs[s, :, 0, :].T
        columns = [table[:CAP, j : j + 1] for j in range(CORES * near)]
        return compare(best, block, columns, queries[0], query_labels, s)

    for s in range(planes):
        collect(0, 0, s)
    query_labels = labels_of(0)
    lowest = jnp.full((8, query_count), -1.0, jnp.float32)
    best = lowest
    for s in range(last):
        for m in range(near):
            wait_recv(across(m, s))
        for n, j in ((1, 1), (2, 2), (3, near + 1)):
            collect(n, j, s)
        if s < last - 1:
            best = own_group(best, s, query_labels)
    forward(last)
    for n, j in ((1, 1), (2, 2)):
        collect(n, j, last)

    def cross(n, block, j):
        columns = [labs[s, :, 0, :].T[:CAP, j : j + 1] for s in range(planes)]
        found = compare(lowest, queries[block], columns, queries[n + 1], labels_of(n + 1), None)
        cross_send[n] = jnp.max(found, axis=0, keepdims=True)
        cross_copy(n).start()

    best = own_group(best, last - 1, query_labels)
    for m in range(near):
        wait_recv(across(m, last))
    collect(3, near + 1, last)
    cross(0, 2, 2)
    cross(1, 3, near + 1)
    best = own_group(best, last, query_labels)
    best = jnp.max(best, axis=0, keepdims=True)
    for n in range(2):
        cross_copy(n).wait_recv()
    best = jnp.maximum(best, jnp.maximum(cross_box[0], cross_box[1]))
    for n in range(planes // 2):
        best_send[n] = best[:, n * 128 : (n + 1) * 128]
    best_box[0] = best[:, :128]
    for d in range(1, planes):
        best_copy(d).start()

    bin_width = 2.0 / (BINS - 1)
    centers = -1.0 + lax.broadcasted_iota(jnp.int32, (BINS, query_count), 0).astype(jnp.float32) * bin_width
    weights = jnp.maximum(1.0 - jnp.abs(best - centers) / bin_width, 0.0)
    filled = jnp.broadcast_to((query_labels >= 0.0).astype(jnp.float32), (8, query_count))
    totals = lax.dot_general(
        filled, weights, (((1,), (1,)), ((), ())), precision=lax.Precision.HIGHEST, preferred_element_type=jnp.float32
    )[0:1]
    hist_send[...] = totals
    hist_box[0, 0] = totals
    for peer in sorted(peers, key=lambda p: -((p[0] > 0) + (p[0] == 3) + (p[2] > 0))):
        hist_copy(*peer).start()

    for d in range(1, planes):
        best_copy(d).wait_recv()
    answers = jnp.concatenate([best_box[d] for d in range(planes)] * (8 // planes), axis=0)
    found = [
        jnp.dot(answers, (wide == rank + n * CAP).astype(jnp.float32), precision=lax.Precision.HIGHEST,
                preferred_element_type=jnp.float32)
        for n in range(2)
    ]
    odd = lax.broadcasted_iota(jnp.int32, (8, docs), 0) % 2 == 1
    best_ref[...] = jnp.sum(jnp.where(member, jnp.where(odd, found[1], found[0]), 0.0), axis=0, keepdims=True)

    for n in range(2):
        cross_copy(n).wait_send()
    for d in range(1, planes):
        wait_send(along_z(d))
        best_copy(d).wait_send()
    for s in range(planes):
        for n in range(4):
            wait_send(hop(n, s))
        for m in range(near):
            wait_send(across(m, s))
    for peer in peers:
        hist_copy(*peer).wait()
    hist_ref[...] = jnp.sum(jnp.sum(hist_box[...], axis=0), axis=0) / doc_total


def plane_shards(embeddings, document_cluster_index):
    rows, cols = lax.axis_size("rows"), lax.axis_size("cols")
    planes = cols // CORES
    docs, width = embeddings.shape
    blocks = CORES * rows
    near = rows - 1
    hbm, vmem = pl.BlockSpec(memory_space=pl.ANY), pl.BlockSpec(memory_space=pltpu.VMEM)
    dma = pltpu.SemaphoreType.DMA
    row = lambda *lead: pltpu.VMEM((*lead, 1, 128), jnp.float32)
    best, histogram = pl.pallas_call(
        functools.partial(plane_kernel, planes, docs * rows * cols),
        out_shape=(pltpu.VMEM((1, docs), jnp.float32), pltpu.VMEM((1, BINS), jnp.float32)),
        in_specs=[hbm, hbm],
        out_specs=(vmem, vmem),
        scratch_shapes=[
            pltpu.VMEM((docs, width), jnp.bfloat16),
            pltpu.VMEM((1, docs), jnp.int32),
            pltpu.VMEM((planes, CORES * near, CAP, width), jnp.bfloat16),
            pltpu.VMEM((planes - 1, CAP, width), jnp.bfloat16),
            pltpu.VMEM((4, planes * CAP, width), jnp.bfloat16),
            row(planes - 1),
            row(planes, 8),
            pltpu.VMEM((2, 1, planes * CAP), jnp.float32),
            pltpu.VMEM((2, 1, planes * CAP), jnp.float32),
            row(planes // 2),
            row(planes),
            row(),
            row(planes, blocks),
            dma((2,)),
            dma((2, 3, planes)),
            dma((2, 4, 2, planes)),
            dma((2, near, 2, planes)),
            dma((2, 2)),
            dma((2, planes)),
            dma((2, planes, blocks)),
        ],
        compiler_params=pltpu.CompilerParams(collective_id=0, has_side_effects=True),
    )(embeddings, document_cluster_index.reshape(1, docs))
    return best.reshape(docs), histogram.reshape(BINS)


def solution(mesh):
    placed = (P(("rows", "cols"), None), P(("rows", "cols")))
    rows, planes = mesh.shape["rows"], mesh.shape["cols"] // CORES
    direct = rows == 4 and planes == rows
    return jax.shard_map(
        plane_shards if direct else shards, mesh=mesh, in_specs=placed,
        out_specs=(P(("rows", "cols")), P()), check_vma=False
    )
```
